32 devices in a mesh: slc: 16 (over z, y, core), col: 2 (over x).
Axes of the slice: x: 2, y: 2, z: 4, core: 2. Of those that a mesh axis runs over, the one named last changes fastest.
Arguments:
- basis: bfloat16 [16, 2, 1152, 3456], P('slc', None, None, 'col'), may hold values from -6 to 6
- picks: int32 [16, 608], P('slc', 'col'), may hold values from 0 to 1727, as said below
- coil_maps: bfloat16 [128, 16, 2, 32, 128], P('slc'), may hold values from -6 to 6
Outputs:
- mapped: bfloat16 [128, 16, 2, 32, 128], P('slc', None, None, 'col')
The draws below stay inside these ranges and needn't reach their ends.
Inputs may be any that keep to these rules, and one draw needn't show every extreme that they name: `picks`: for each slice, the entries in each of the 2 blocks of 304 positions are distinct offsets within the corresponding block of 1728 calibration windows.
All inputs are finite; a program needn't handle non-finite values.
Results may differ from the reference program's by a relative error of at most 0.0049.
Values may be sent and summed in bfloat16 or wider, within the bound.
A program may use at most 448 MiB of HBM per device.

```python
import math
import jax
import jax.numpy as jnp
from jax import lax

COILS = 32
KSIZE = 6
NCOL = 3456
RANK = 608
IMG = 128
ROWS = 1152
SLICES = 16
N_COL = 2


def draw_picks(key, part):
    block_cols = NCOL // N_COL
    keep_cols = RANK // N_COL
    keys = jax.random.split(jax.random.fold_in(key, 7), SLICES * N_COL)
    chosen = jax.vmap(lambda one_key: jax.random.permutation(one_key, block_cols)[:keep_cols])(keys)
    return chosen.reshape(SLICES, RANK).astype(jnp.int32)


def block_levels(own_key, shape, shards, smallest, high):
    def one(position, parts):
        heights = jax.random.uniform(jax.random.fold_in(jax.random.fold_in(own_key, 6), position), (parts,), jnp.float32, smallest / len(shards), high / len(shards))
        return jnp.repeat(jnp.exp(heights), shape[position] // parts).reshape((-1,) + (1,) * (len(shape) - position - 1))

    factor_of = one(*shards[0])
    for cut in shards[1:]:
        factor_of = factor_of * one(*cut)
    return factor_of


def scatter_about(rng, shape, scale, bound, pieces=(), held_as=jnp.bfloat16):
    values = scale * jax.random.normal(rng, shape, jnp.float32)
    if pieces:
        values = values * block_levels(rng, shape, pieces, -0.22, 0.18)
    return jnp.clip(values, -bound, bound).astype(held_as)


def setup_inputs(seed: int = 0) -> dict:
    key_list = jax.random.split(jax.random.key(seed), 4)
    basis = scatter_about(key_list[0], (SLICES, 2, ROWS, NCOL), 1.0, 6.0, ((0, 16), (3, 2)))
    picks = draw_picks(jax.random.fold_in(key_list[3], 71), 0)
    coil_maps = scatter_about(key_list[2], (IMG, SLICES, 2, COILS, IMG), 1.0, 6.0, ((0, 16),))
    return dict(basis=basis, picks=picks, coil_maps=coil_maps)


def phase_tables(span, length):
    centre = (span - 1) // 2
    offsets = jnp.arange(span).astype(jnp.int32) - centre
    columns = jnp.arange(length).astype(jnp.int32)
    turns = (offsets[:, None] * columns[None, :]) % length
    angles = turns.astype(jnp.float32) * (2.0 * math.pi / length)
    return jnp.cos(angles), jnp.sin(angles)


def shift_table(count):
    first = jnp.arange(count).astype(jnp.int32)[:, None, None]
    second = jnp.arange(count).astype(jnp.int32)[None, :, None]
    target = jnp.arange(2 * count - 1).astype(jnp.int32)[None, None, :]
    return (second - first + count - 1 == target).astype(jnp.float32)


def slice_gram(values_in):
    real_part = jnp.dot(values_in[0], values_in[0].T, preferred_element_type=jnp.float32) + jnp.dot(values_in[1], values_in[1].T, preferred_element_type=jnp.float32)
    imag_part = jnp.dot(values_in[1], values_in[0].T, preferred_element_type=jnp.float32) - jnp.dot(values_in[0], values_in[1].T, preferred_element_type=jnp.float32)
    return jnp.stack([real_part, imag_part])


def kernel_sums(gram):
    blocks = gram.reshape(2, COILS, KSIZE, KSIZE, COILS, KSIZE, KSIZE)
    shifts = shift_table(KSIZE)
    return jnp.einsum("rcaxdby,abp,xyq->rcdpq", blocks, shifts, shifts, precision=lax.Precision.HIGHEST)


def column_transform(kernels, cos_table, sin_table, factor):
    def apply_table(values_in, table):
        return jnp.einsum("cdpq,qy->ycdp", values_in, table, precision=lax.Precision.HIGHEST)
    real_part = apply_table(kernels[0], cos_table) - apply_table(kernels[1], sin_table)
    imag_part = apply_table(kernels[0], sin_table) + apply_table(kernels[1], cos_table)
    return (jnp.stack([real_part, imag_part], axis=1) * factor).astype(jnp.bfloat16)


def apply_maps(rows_q, maps_one, cos_table, sin_table):
    kernel_f = rows_q.astype(jnp.float32)
    maps_f = maps_one.astype(jnp.float32)

    def product(left_op, right_op):
        return jnp.einsum("ycdp,ydx->ycpx", left_op, right_op, precision=lax.Precision.HIGHEST)
    mixed_real = product(kernel_f[:, 0], maps_f[:, 0]) - product(kernel_f[:, 1], maps_f[:, 1])
    mixed_imag = product(kernel_f[:, 0], maps_f[:, 1]) + product(kernel_f[:, 1], maps_f[:, 0])

    def apply_table(values_in, table):
        return jnp.einsum("ycpx,px->ycx", values_in, table, precision=lax.Precision.HIGHEST)
    out_real = apply_table(mixed_real, cos_table) - apply_table(mixed_imag, sin_table)
    out_imag = apply_table(mixed_real, sin_table) + apply_table(mixed_imag, cos_table)
    return jnp.stack([out_real, out_imag], axis=1).astype(jnp.bfloat16)


def reference(basis, picks, coil_maps):
    block_cols = NCOL // N_COL
    keep_cols = RANK // N_COL
    offsets = (jnp.arange(RANK).astype(jnp.int32) // keep_cols) * block_cols
    span = 2 * KSIZE - 1
    cos_table, sin_table = phase_tables(span, IMG)
    factor = 1.0 / (2.0 * RANK * KSIZE * KSIZE)
    maps_first = jnp.transpose(coil_maps, (1, 0, 2, 3, 4))

    def per_slice(inputs):
        values_in, columns, maps_one = inputs
        picked = jnp.take(values_in, columns.astype(jnp.int32) + offsets, axis=2)
        gram = slice_gram(picked)
        kernels = kernel_sums(gram)
        rows_q = column_transform(kernels, cos_table, sin_table, factor)
        return apply_maps(rows_q, maps_one, cos_table, sin_table)

    results = lax.map(per_slice, (basis, picks, maps_first))
    return jnp.transpose(results, (1, 0, 2, 3, 4))
```

```python
import functools
import math

import jax
import jax.numpy as jnp
from jax import lax
from jax.experimental import pallas as pl
from jax.experimental.pallas import tpu as pltpu
from jax.sharding import PartitionSpec as P

COILS = 32
KSIZE = 6
SPAN = 2 * KSIZE - 1
SLOTS = SPAN + 1
CENTRE = KSIZE - 1
PAIR = 2 * COILS


def dot_nn(left, right):
    return jnp.dot(left, right, preferred_element_type=jnp.float32)


def dot_nt(left, right):
    return lax.dot_general(
        left, right, (((1,), (1,)), ((), ())), preferred_element_type=jnp.float32
    )


def gram_kernel(
    factor, share, col_ref, basis_ref, picks_ref, own_ref, other_ref, hot, order, x, xa, xb, yr, yi, tacc
):
    keep, block = hot.shape
    rows = order.shape[0]
    side = KSIZE * share
    parts = COILS // share
    lanes = lax.broadcasted_iota(jnp.int32, (keep, block), 1)
    hot[...] = (lanes == picks_ref[...]).astype(jnp.float32).astype(jnp.bfloat16)
    source = lax.broadcasted_iota(jnp.int32, (COILS, rows), 1)
    coil = lax.broadcasted_iota(jnp.int32, (COILS, rows), 0)
    gap = source - coil * (KSIZE * KSIZE)

    def fill(spot, carry):
        at = pl.multiple_of(spot * COILS, COILS)
        order[pl.ds(at, COILS), :] = (gap == spot).astype(jnp.float32).astype(jnp.bfloat16)
        return carry

    lax.fori_loop(0, KSIZE * KSIZE, fill, 0)
    chunk = KSIZE * COILS

    def choose(ri, carry):
        windows = dot_nn(hot[...], basis_ref[ri]).astype(jnp.bfloat16)

        def permute(step, inner):
            at = pl.multiple_of(step * chunk, chunk)
            x[ri, pl.ds(at, chunk), :] = dot_nt(order[pl.ds(at, chunk), :], windows).astype(
                jnp.bfloat16
            )
            return inner

        return lax.fori_loop(0, rows // chunk, permute, carry)

    lax.fori_loop(0, 2, choose, 0)

    zeros = jnp.zeros((PAIR, keep), jnp.bfloat16)
    for a in range(KSIZE):
        for ref in (xa, xb):
            ref[a, :PAIR, :] = zeros
            ref[a, (KSIZE + 1) * PAIR :, :] = zeros
        for b in range(KSIZE):
            at = (a * KSIZE + b) * COILS
            to = (b + 1) * PAIR
            real = x[0, at : at + COILS, :]
            imag = x[1, at : at + COILS, :]
            xa[a, to : to + COILS, :] = real
            xa[a, to + COILS : to + PAIR, :] = -imag
            xb[a, to : to + COILS, :] = imag
            xb[a, to + COILS : to + PAIR, :] = real
            for h in range(parts):
                row = h * side + a * share
                yr[b, row : row + share, :] = x[0, at + h * share : at + (h + 1) * share, :]
                yi[b, row : row + share, :] = x[1, at + h * share : at + (h + 1) * share, :]

    def blocks(a2, carry):
        tacc[a2] = jnp.zeros(tacc.shape[1:], jnp.float32)
        for b in range(KSIZE):
            if (CENTRE - b) % 2 == 0:
                low, high, off = PAIR, (KSIZE + 1) * PAIR, (CENTRE - b) * PAIR
            else:
                low, high, off = 0, (KSIZE + 2) * PAIR, (CENTRE - 1 - b) * PAIR
            tacc[a2, :, off : off + high - low] += dot_nt(yr[b], xa[a2, low:high, :]) + dot_nt(
                yi[b], xb[a2, low:high, :]
            )
        return carry

    lax.fori_loop(0, KSIZE, blocks, 0)

    own = col_ref[0]
    for ref, part in ((own_ref, own), (other_ref, parts - 1 - own)):
        for p in range(SPAN):
            total = None
            for a in range(max(0, CENTRE - p), min(KSIZE, KSIZE + CENTRE - p)):
                at = pl.multiple_of(part * side + a * share, share)
                term = tacc[a + p - CENTRE, pl.ds(at, share), :]
                total = term if total is None else total + term
            ref[p * share : (p + 1) * share, :] = total * factor


def join_kernel(own_ref, got_ref, out_ref):
    total = own_ref[...] + got_ref[...]
    high = total.astype(jnp.bfloat16)
    left = total - high.astype(jnp.float32)
    last = SPAN * PAIR
    out_ref[...] = high
    mid = CENTRE * PAIR
    out_ref[:, last:] = left[:, mid : mid + PAIR].astype(jnp.bfloat16)


def apply_kernel(
    width, share, kernels_ref, phase_ref, cos_ref, sin_ref, maps_ref, out_ref, high, low
):
    @pl.when(pl.program_id(0) == 0)
    def _():
        phase = phase_ref[...]
        phase_high = phase.astype(jnp.bfloat16)
        phase_low = (phase - phase_high.astype(jnp.float32)).astype(jnp.bfloat16)
        from_lane = lax.broadcasted_iota(jnp.int32, (phase.shape[1], width * PAIR), 0)
        to_lane = lax.broadcasted_iota(jnp.int32, (phase.shape[1], width * PAIR), 1)
        spread = (from_lane == to_lane // COILS).astype(jnp.float32).astype(jnp.bfloat16)
        row = lax.broadcasted_iota(jnp.int32, high.shape, 0)
        lane = lax.broadcasted_iota(jnp.int32, high.shape, 1)
        same = row % COILS == lane % COILS
        high[...] = jnp.where(same, dot_nn(phase_high, spread), 0.0).astype(jnp.bfloat16)
        low[...] = jnp.where(same, dot_nn(phase_low, spread), 0.0).astype(jnp.bfloat16)

    kernels = kernels_ref[0]
    image = (dot_nn(kernels, high[...]) + dot_nn(kernels, low[...])).astype(jnp.bfloat16)
    cos_x = cos_ref[...]
    sin_x = sin_ref[...]
    length = cos_x.shape[1]
    for y in range(width):
        real = maps_ref[y, 0, 0]
        imag = maps_ref[y, 0, 1]
        both = jnp.concatenate(
            [jnp.concatenate([real, imag], axis=1), jnp.concatenate([-imag, real], axis=1)], axis=0
        )
        mixed = dot_nn(image[:, y * PAIR : (y + 1) * PAIR], both)
        mixed_real = mixed[:, :length]
        mixed_imag = mixed[:, length:]
        out_real = mixed_real * cos_x - mixed_imag * sin_x
        out_imag = mixed_real * sin_x + mixed_imag * cos_x
        for ri, value in ((0, out_real), (1, out_imag)):
            total = value[:share]
            for p in range(1, SPAN):
                total = total + value[p * share : (p + 1) * share]
            out_ref[y, 0, ri] = total.astype(jnp.bfloat16)


def shards(basis, picks, coil_maps):
    n_col = lax.axis_size("col")
    share = COILS // n_col
    length = coil_maps.shape[-1]
    width = coil_maps.shape[0]
    slices = coil_maps.shape[1]
    rows, block = basis.shape[2:]
    keep = picks.shape[1]
    factor = 1.0 / (2.0 * keep * n_col * KSIZE * KSIZE)
    high_rows = SPAN * share
    lanes = SLOTS * PAIR
    vmem = pl.BlockSpec(memory_space=pltpu.VMEM)
    bf16 = jnp.bfloat16

    windows = jnp.transpose(basis[0], (0, 2, 1))
    col = lax.axis_index("col").astype(jnp.int32).reshape(1)
    part = jax.ShapeDtypeStruct((high_rows, lanes), jnp.float32)
    own, other = pl.pallas_call(
        functools.partial(gram_kernel, factor, share),
        out_shape=(part, part),
        in_specs=[pl.BlockSpec(memory_space=pltpu.SMEM), vmem, vmem],
        out_specs=(vmem, vmem),
        scratch_shapes=[
            pltpu.VMEM((keep, block), bf16),
            pltpu.VMEM((rows, rows), bf16),
            pltpu.VMEM((2, rows, keep), bf16),
            pltpu.VMEM((KSIZE, (KSIZE + 2) * PAIR, keep), bf16),
            pltpu.VMEM((KSIZE, (KSIZE + 2) * PAIR, keep), bf16),
            pltpu.VMEM((KSIZE, KSIZE * COILS, keep), bf16),
            pltpu.VMEM((KSIZE, KSIZE * COILS, keep), bf16),
            pltpu.VMEM((KSIZE, KSIZE * COILS, lanes), jnp.float32),
        ],
        compiler_params=pltpu.CompilerParams(vmem_limit_bytes=60 * 2**20),
        name="gram",
    )(col, windows, picks.reshape(keep, 1))

    got = lax.ppermute(other, "col", [(i, n_col - 1 - i) for i in range(n_col)])
    kernels = pl.pallas_call(
        join_kernel,
        out_shape=jax.ShapeDtypeStruct((high_rows, lanes), bf16),
        in_specs=[vmem, vmem],
        out_specs=vmem,
        name="join",
    )(own, got)
    gathered = lax.all_gather(kernels, "slc", axis=0)

    row = lax.broadcasted_iota(jnp.int32, (lanes, 128), 0)
    lane = lax.broadcasted_iota(jnp.int32, (lanes, 128), 1)
    slot = row // PAIR
    offset = jnp.where(slot == SPAN, 0, slot - CENTRE)
    column = lax.axis_index("slc") * width + lane // 2
    angle = (offset * column % length).astype(jnp.float32) * (2.0 * math.pi / length)
    from_imag = row // COILS % 2
    to_imag = lane % 2
    phase = jnp.where(from_imag == to_imag, jnp.cos(angle), jnp.sin(angle))
    phase = jnp.where((from_imag == 1) & (to_imag == 0), -phase, phase)

    spot = lax.broadcasted_iota(jnp.int32, (high_rows, length), 0) // share - CENTRE
    place = lax.broadcasted_iota(jnp.int32, (high_rows, length), 1)
    turn = (spot * place % length).astype(jnp.float32) * (2.0 * math.pi / length)

    whole = lambda shape: pl.BlockSpec(shape, lambda s: (0,) * len(shape))
    return pl.pallas_call(
        functools.partial(apply_kernel, width, share),
        grid=(slices,),
        out_shape=jax.ShapeDtypeStruct((width, slices, 2, share, length), bf16),
        in_specs=[
            pl.BlockSpec((1, high_rows, lanes), lambda s: (s, 0, 0)),
            whole((lanes, 128)),
            whole((high_rows, length)),
            whole((high_rows, length)),
            pl.BlockSpec((width, 1, 2, COILS, length), lambda s: (0, s, 0, 0, 0)),
        ],
        out_specs=pl.BlockSpec((width, 1, 2, share, length), lambda s: (0, s, 0, 0, 0)),
        scratch_shapes=[
            pltpu.VMEM((lanes, width * PAIR), bf16),
            pltpu.VMEM((lanes, width * PAIR), bf16),
        ],
        name="apply",
    )(gathered, phase, jnp.cos(turn), jnp.sin(turn), coil_maps)


def solution(mesh):
    placed = (P("slc", None, None, "col"), P("slc", "col"), P("slc", None, None, None, None))
    return jax.shard_map(
        shards,
        mesh=mesh,
        in_specs=placed,
        out_specs=P("slc", None, None, "col", None),
        check_vma=False,
    )
```

```python
import functools
import math

import jax
import jax.numpy as jnp
from jax import lax
from jax.experimental import pallas as pl
from jax.experimental.pallas import tpu as pltpu
from jax.sharding import PartitionSpec as P

COILS = 32
KSIZE = 6
SPAN = 2 * KSIZE - 1
SLOTS = SPAN + 1
CENTRE = KSIZE - 1
PAIR = 2 * COILS


def dot_nn(left, right):
    return jnp.dot(left, right, preferred_element_type=jnp.float32)


def dot_nt(left, right):
    return lax.dot_general(
        left, right, (((1,), (1,)), ((), ())), preferred_element_type=jnp.float32
    )


def gram_kernel(
    factor, share, col_ref, basis_ref, picks_ref, own_ref, other_ref, hot, order, x, xa, xb, yr, yi, tacc
):
    keep, block = hot.shape
    rows = order.shape[0]
    side = KSIZE * share
    parts = COILS // share
    lanes = lax.broadcasted_iota(jnp.int32, (keep, block), 1)
    hot[...] = (lanes == picks_ref[...]).astype(jnp.float32).astype(jnp.bfloat16)
    source = lax.broadcasted_iota(jnp.int32, (COILS, rows), 1)
    coil = lax.broadcasted_iota(jnp.int32, (COILS, rows), 0)
    gap = source - coil * (KSIZE * KSIZE)

    def fill(spot, carry):
        at = pl.multiple_of(spot * COILS, COILS)
        order[pl.ds(at, COILS), :] = (gap == spot).astype(jnp.float32).astype(jnp.bfloat16)
        return carry

    lax.fori_loop(0, KSIZE * KSIZE, fill, 0)
    chunk = KSIZE * COILS

    def choose(ri, carry):
        windows = dot_nn(hot[...], basis_ref[ri]).astype(jnp.bfloat16)

        def permute(step, inner):
            at = pl.multiple_of(step * chunk, chunk)
            x[ri, pl.ds(at, chunk), :] = dot_nt(order[pl.ds(at, chunk), :], windows).astype(
                jnp.bfloat16
            )
            return inner

        return lax.fori_loop(0, rows // chunk, permute, carry)

    lax.fori_loop(0, 2, choose, 0)

    zeros = jnp.zeros((PAIR, keep), jnp.bfloat16)
    for a in range(KSIZE):
        for ref in (xa, xb):
            ref[a, :PAIR, :] = zeros
            ref[a, (KSIZE + 1) * PAIR :, :] = zeros
        for b in range(KSIZE):
            at = (a * KSIZE + b) * COILS
            to = (b + 1) * PAIR
            real = x[0, at : at + COILS, :]
            imag = x[1, at : at + COILS, :]
            xa[a, to : to + COILS, :] = real
            xa[a, to + COILS : to + PAIR, :] = -imag
            xb[a, to : to + COILS, :] = imag
            xb[a, to + COILS : to + PAIR, :] = real
            for h in range(parts):
                row = h * side + a * share
                yr[b, row : row + share, :] = x[0, at + h * share : at + (h + 1) * share, :]
                yi[b, row : row + share, :] = x[1, at + h * share : at + (h + 1) * share, :]

    def blocks(a2, carry):
        tacc[a2] = jnp.zeros(tacc.shape[1:], jnp.float32)
        for b in range(KSIZE):
            if (CENTRE - b) % 2 == 0:
                low, high, off = PAIR, (KSIZE + 1) * PAIR, (CENTRE - b) * PAIR
            else:
                low, high, off = 0, (KSIZE + 2) * PAIR, (CENTRE - 1 - b) * PAIR
            tacc[a2, :, off : off + high - low] += dot_nt(yr[b], xa[a2, low:high, :]) + dot_nt(
                yi[b], xb[a2, low:high, :]
            )
        return carry

    lax.fori_loop(0, KSIZE, blocks, 0)

    own = col_ref[0]
    for ref, part in ((own_ref, own), (other_ref, parts - 1 - own)):
        for p in range(SPAN):
            total = None
            for a in range(max(0, CENTRE - p), min(KSIZE, KSIZE + CENTRE - p)):
                at = pl.multiple_of(part * side + a * share, share)
                term = tacc[a + p - CENTRE, pl.ds(at, share), :]
                total = term if total is None else total + term
            ref[p * share : (p + 1) * share, :] = total * factor


def join_kernel(own_ref, got_ref, out_ref):
    total = own_ref[...] + got_ref[...]
    high = total.astype(jnp.bfloat16)
    left = total - high.astype(jnp.float32)
    last = SPAN * PAIR
    out_ref[...] = high
    mid = CENTRE * PAIR
    out_ref[:, last:] = left[:, mid : mid + PAIR].astype(jnp.bfloat16)


def spread_kernel(in_ref, out_ref, local_sem, send, got):
    chips = lax.axis_size("slc") // 2
    me = lax.axis_index("slc")
    core = me % 2
    column = me // 2 // 2
    side = me // 2 % 2
    spot = column + side * (chips - 1 - 2 * column)

    def at(position):
        position = (position + 2 * chips) % chips
        far = position // (chips // 2)
        near = position + far * (chips - 1 - 2 * position)
        return (2 * near + far) * 2 + core

    ahead, behind, twin = at(spot + 1), at(spot - 1), me + 1 - 2 * core
    barrier = pltpu.get_barrier_semaphore()
    for peer in (ahead, behind, twin):
        pl.semaphore_signal(
            barrier, inc=1, device_id={"slc": peer}, device_id_type=pl.DeviceIdType.MESH
        )
    pl.semaphore_wait(barrier, 3)

    forward = chips // 2
    backward = chips - 1 - forward
    rows = in_ref.shape[0]
    cut = (rows // 2 + 15) // 16 * 16
    pieces = ((0, cut), (cut, rows - cut))
    ring_ahead, ring_behind, across = 0, forward, forward + backward

    def copy(source, slot, piece, index, peer):
        start, size = pieces[piece]
        target = out_ref.at[slot, pl.ds(start, size), :]
        taken = target if source is None else source.at[pl.ds(start, size), :]
        return pltpu.make_async_remote_copy(
            src_ref=taken,
            dst_ref=target,
            send_sem=send.at[index, piece],
            recv_sem=got.at[index, piece],
            device_id={"slc": peer},
            device_id_type=pl.DeviceIdType.MESH,
        )

    local = pltpu.make_async_copy(in_ref, out_ref.at[me], local_sem)
    sent = []

    def launch(*what):
        one = copy(*what)
        one.start()
        sent.append(one)

    for piece in range(2):
        launch(in_ref, me, piece, ring_ahead, ahead)
        launch(in_ref, me, piece, ring_behind, behind)
    for piece in range(2):
        launch(in_ref, me, piece, across, twin)
    local.start()
    for step in range(forward):
        for piece in range(2):
            slot = at(spot - 1 - step)
            copy(None, slot, piece, ring_ahead + step, behind).wait_recv()
            if step + 1 < forward:
                launch(None, slot, piece, ring_ahead + step + 1, ahead)
            launch(None, slot, piece, across + 1 + step, twin)
            if step < backward:
                slot = at(spot + 1 + step)
                copy(None, slot, piece, ring_behind + step, ahead).wait_recv()
                if step + 1 < backward:
                    launch(None, slot, piece, ring_behind + step + 1, behind)
                launch(None, slot, piece, across + 1 + forward + step, twin)
    for index in range(chips):
        for piece in range(2):
            if index == 0:
                slot = twin
            elif index <= forward:
                slot = at(spot - index) + 1 - 2 * core
            else:
                slot = at(spot + index - forward) + 1 - 2 * core
            copy(None, slot, piece, across + index, twin).wait_recv()
    for one in sent:
        one.wait_send()
    local.wait()


def apply_kernel(
    width, share, kernels_ref, phase_ref, cos_ref, sin_ref, maps_ref, out_ref, high, low
):
    @pl.when(pl.program_id(0) == 0)
    def _():
        phase = phase_ref[...]
        phase_high = phase.astype(jnp.bfloat16)
        phase_low = (phase - phase_high.astype(jnp.float32)).astype(jnp.bfloat16)
        from_lane = lax.broadcasted_iota(jnp.int32, (phase.shape[1], width * PAIR), 0)
        to_lane = lax.broadcasted_iota(jnp.int32, (phase.shape[1], width * PAIR), 1)
        spread = (from_lane == to_lane // COILS).astype(jnp.float32).astype(jnp.bfloat16)
        row = lax.broadcasted_iota(jnp.int32, high.shape, 0)
        lane = lax.broadcasted_iota(jnp.int32, high.shape, 1)
        same = row % COILS == lane % COILS
        high[...] = jnp.where(same, dot_nn(phase_high, spread), 0.0).astype(jnp.bfloat16)
        low[...] = jnp.where(same, dot_nn(phase_low, spread), 0.0).astype(jnp.bfloat16)

    kernels = kernels_ref[0]
    image = (dot_nn(kernels, high[...]) + dot_nn(kernels, low[...])).astype(jnp.bfloat16)
    cos_x = cos_ref[...]
    sin_x = sin_ref[...]
    length = cos_x.shape[1]
    for y in range(width):
        real = maps_ref[y, 0, 0]
        imag = maps_ref[y, 0, 1]
        both = jnp.concatenate(
            [jnp.concatenate([real, imag], axis=1), jnp.concatenate([-imag, real], axis=1)], axis=0
        )
        mixed = dot_nn(image[:, y * PAIR : (y + 1) * PAIR], both)
        mixed_real = mixed[:, :length]
        mixed_imag = mixed[:, length:]
        out_real = mixed_real * cos_x - mixed_imag * sin_x
        out_imag = mixed_real * sin_x + mixed_imag * cos_x
        for ri, value in ((0, out_real), (1, out_imag)):
            total = value[:share]
            for p in range(1, SPAN):
                total = total + value[p * share : (p + 1) * share]
            out_ref[y, 0, ri] = total.astype(jnp.bfloat16)


def shards(basis, picks, coil_maps):
    n_col = lax.axis_size("col")
    share = COILS // n_col
    length = coil_maps.shape[-1]
    width = coil_maps.shape[0]
    slices = coil_maps.shape[1]
    rows, block = basis.shape[2:]
    keep = picks.shape[1]
    factor = 1.0 / (2.0 * keep * n_col * KSIZE * KSIZE)
    high_rows = SPAN * share
    lanes = SLOTS * PAIR
    vmem = pl.BlockSpec(memory_space=pltpu.VMEM)
    bf16 = jnp.bfloat16

    windows = jnp.transpose(basis[0], (0, 2, 1))
    col = lax.axis_index("col").astype(jnp.int32).reshape(1)
    part = jax.ShapeDtypeStruct((high_rows, lanes), jnp.float32)
    own, other = pl.pallas_call(
        functools.partial(gram_kernel, factor, share),
        out_shape=(part, part),
        in_specs=[pl.BlockSpec(memory_space=pltpu.SMEM), vmem, vmem],
        out_specs=(vmem, vmem),
        scratch_shapes=[
            pltpu.VMEM((keep, block), bf16),
            pltpu.VMEM((rows, rows), bf16),
            pltpu.VMEM((2, rows, keep), bf16),
            pltpu.VMEM((KSIZE, (KSIZE + 2) * PAIR, keep), bf16),
            pltpu.VMEM((KSIZE, (KSIZE + 2) * PAIR, keep), bf16),
            pltpu.VMEM((KSIZE, KSIZE * COILS, keep), bf16),
            pltpu.VMEM((KSIZE, KSIZE * COILS, keep), bf16),
            pltpu.VMEM((KSIZE, KSIZE * COILS, lanes), jnp.float32),
        ],
        compiler_params=pltpu.CompilerParams(vmem_limit_bytes=60 * 2**20),
        name="gram",
    )(col, windows, picks.reshape(keep, 1))

    got = lax.ppermute(other, "col", [(i, n_col - 1 - i) for i in range(n_col)])
    kernels = pl.pallas_call(
        join_kernel,
        out_shape=jax.ShapeDtypeStruct((high_rows, lanes), bf16),
        in_specs=[vmem, vmem],
        out_specs=vmem,
        name="join",
    )(own, got)
    n_slc = lax.axis_size("slc")
    gathered = pl.pallas_call(
        spread_kernel,
        out_shape=jax.ShapeDtypeStruct((n_slc, high_rows, lanes), bf16),
        in_specs=[vmem],
        out_specs=pl.BlockSpec(memory_space=pl.ANY),
        scratch_shapes=[
            pltpu.SemaphoreType.DMA,
            pltpu.SemaphoreType.DMA((n_slc - 1, 2)),
            pltpu.SemaphoreType.DMA((n_slc - 1, 2)),
        ],
        compiler_params=pltpu.CompilerParams(collective_id=0, has_side_effects=True),
        name="spread",
    )(kernels)

    row = lax.broadcasted_iota(jnp.int32, (lanes, 128), 0)
    lane = lax.broadcasted_iota(jnp.int32, (lanes, 128), 1)
    slot = row // PAIR
    offset = jnp.where(slot == SPAN, 0, slot - CENTRE)
    column = lax.axis_index("slc") * width + lane // 2
    angle = (offset * column % length).astype(jnp.float32) * (2.0 * math.pi / length)
    from_imag = row // COILS % 2
    to_imag = lane % 2
    phase = jnp.where(from_imag == to_imag, jnp.cos(angle), jnp.sin(angle))
    phase = jnp.where((from_imag == 1) & (to_imag == 0), -phase, phase)

    spot = lax.broadcasted_iota(jnp.int32, (high_rows, length), 0) // share - CENTRE
    place = lax.broadcasted_iota(jnp.int32, (high_rows, length), 1)
    turn = (spot * place % length).astype(jnp.float32) * (2.0 * math.pi / length)

    whole = lambda shape: pl.BlockSpec(shape, lambda s: (0,) * len(shape))
    return pl.pallas_call(
        functools.partial(apply_kernel, width, share),
        grid=(slices,),
        out_shape=jax.ShapeDtypeStruct((width, slices, 2, share, length), bf16),
        in_specs=[
            pl.BlockSpec((1, high_rows, lanes), lambda s: (s, 0, 0)),
            whole((lanes, 128)),
            whole((high_rows, length)),
            whole((high_rows, length)),
            pl.BlockSpec((width, 1, 2, COILS, length), lambda s: (0, s, 0, 0, 0)),
        ],
        out_specs=pl.BlockSpec((width, 1, 2, share, length), lambda s: (0, s, 0, 0, 0)),
        scratch_shapes=[
            pltpu.VMEM((lanes, width * PAIR), bf16),
            pltpu.VMEM((lanes, width * PAIR), bf16),
        ],
        name="apply",
    )(gathered, phase, jnp.cos(turn), jnp.sin(turn), coil_maps)


def solution(mesh):
    placed = (P("slc", None, None, "col"), P("slc", "col"), P("slc", None, None, None, None))
    return jax.shard_map(
        shards,
        mesh=mesh,
        in_specs=placed,
        out_specs=P("slc", None, None, "col", None),
        check_vma=False,
    )
```

```python
import functools
import math

import jax
import jax.numpy as jnp
from jax import lax
from jax.experimental import pallas as pl
from jax.experimental.pallas import tpu as pltpu
from jax.sharding import PartitionSpec as P

COILS = 32
KSIZE = 6
SPAN = 2 * KSIZE - 1
SLOTS = SPAN + 1
CENTRE = KSIZE - 1
PAIR = 2 * COILS


def dot_nn(left, right):
    return jnp.dot(left, right, preferred_element_type=jnp.float32)


def dot_nt(left, right):
    return lax.dot_general(
        left, right, (((1,), (1,)), ((), ())), preferred_element_type=jnp.float32
    )


def store_split(ref, rows, total):
    high = total.astype(jnp.bfloat16)
    last = SPAN * PAIR
    mid = CENTRE * PAIR
    left = total[:, mid : mid + PAIR] - high[:, mid : mid + PAIR].astype(jnp.float32)
    ref[rows, :last] = high[:, :last]
    ref[rows, last:] = left.astype(jnp.bfloat16)


def gram_kernel(
    factor, share, col_ref, basis_ref, picks_ref, own_ref, other_ref, windows_in, sems, hot, order, x, xa, xb, yr, yi, tacc
):
    keep, block = hot.shape
    rows = order.shape[0]
    side = KSIZE * share
    parts = COILS // share
    loads = [
        pltpu.make_async_copy(basis_ref.at[ri], windows_in.at[ri], sems.at[ri]) for ri in range(2)
    ]
    for load in loads:
        load.start()
    lanes = lax.broadcasted_iota(jnp.int32, (keep, block), 1)
    hot[...] = (lanes == picks_ref[...]).astype(jnp.float32).astype(jnp.bfloat16)
    source = lax.broadcasted_iota(jnp.int32, (COILS, rows), 1)
    coil = lax.broadcasted_iota(jnp.int32, (COILS, rows), 0)
    gap = source - coil * (KSIZE * KSIZE)

    def fill(spot, carry):
        at = pl.multiple_of(spot * COILS, COILS)
        order[pl.ds(at, COILS), :] = (gap == spot).astype(jnp.float32).astype(jnp.bfloat16)
        return carry

    lax.fori_loop(0, KSIZE * KSIZE, fill, 0)
    chunk = KSIZE * COILS

    def choose(ri, carry):
        windows = dot_nn(hot[...], windows_in[ri]).astype(jnp.bfloat16)

        def permute(step, inner):
            at = pl.multiple_of(step * chunk, chunk)
            x[ri, pl.ds(at, chunk), :] = dot_nt(order[pl.ds(at, chunk), :], windows).astype(
                jnp.bfloat16
            )
            return inner

        return lax.fori_loop(0, rows // chunk, permute, carry)

    for ri, load in enumerate(loads):
        load.wait()
        choose(ri, 0)

    zeros = jnp.zeros((PAIR, keep), jnp.bfloat16)
    for a in range(KSIZE):
        for ref in (xa, xb):
            ref[a, :PAIR, :] = zeros
            ref[a, (KSIZE + 1) * PAIR :, :] = zeros
        for b in range(KSIZE):
            at = (a * KSIZE + b) * COILS
            to = (b + 1) * PAIR
            real = x[0, at : at + COILS, :]
            imag = x[1, at : at + COILS, :]
            xa[a, to : to + COILS, :] = real
            xa[a, to + COILS : to + PAIR, :] = -imag
            xb[a, to : to + COILS, :] = imag
            xb[a, to + COILS : to + PAIR, :] = real
            for h in range(parts):
                row = h * side + a * share
                yr[b, row : row + share, :] = x[0, at + h * share : at + (h + 1) * share, :]
                yi[b, row : row + share, :] = x[1, at + h * share : at + (h + 1) * share, :]

    def blocks(a2, carry):
        tacc[a2] = jnp.zeros(tacc.shape[1:], jnp.float32)
        for b in range(KSIZE):
            if (CENTRE - b) % 2 == 0:
                low, high, off = PAIR, (KSIZE + 1) * PAIR, (CENTRE - b) * PAIR
            else:
                low, high, off = 0, (KSIZE + 2) * PAIR, (CENTRE - 1 - b) * PAIR
            tacc[a2, :, off : off + high - low] += dot_nt(yr[b], xa[a2, low:high, :]) + dot_nt(
                yi[b], xb[a2, low:high, :]
            )
        return carry

    lax.fori_loop(0, KSIZE, blocks, 0)

    own = col_ref[0]
    for ref, part in ((own_ref, own), (other_ref, parts - 1 - own)):
        for p in range(SPAN):
            total = None
            for a in range(max(0, CENTRE - p), min(KSIZE, KSIZE + CENTRE - p)):
                at = pl.multiple_of(part * side + a * share, share)
                term = tacc[a + p - CENTRE, pl.ds(at, share), :]
                total = term if total is None else total + term
            total = total * factor
            if part is own:
                ref[p * share : (p + 1) * share, :] = total
            else:
                store_split(ref, slice(p * share, (p + 1) * share), total)


def join_kernel(own_ref, got_ref, out_ref, total):
    last = SPAN * PAIR
    mid = CENTRE * PAIR
    total[...] = own_ref[...] + got_ref[...].astype(jnp.float32)
    total[:, mid : mid + PAIR] += got_ref[:, last:].astype(jnp.float32)
    store_split(out_ref, slice(None), total[...])


def spread_kernel(in_ref, out_ref, local_sem, send, got):
    chips = lax.axis_size("slc") // 2
    me = lax.axis_index("slc")
    core = me % 2
    column = me // 2 // 2
    side = me // 2 % 2
    spot = column + side * (chips - 1 - 2 * column)

    def at(position):
        position = (position + 2 * chips) % chips
        far = position // (chips // 2)
        near = position + far * (chips - 1 - 2 * position)
        return (2 * near + far) * 2 + core

    ahead, behind, twin = at(spot + 1), at(spot - 1), me + 1 - 2 * core
    barrier = pltpu.get_barrier_semaphore()
    for peer in (ahead, behind, twin):
        pl.semaphore_signal(
            barrier, inc=1, device_id={"slc": peer}, device_id_type=pl.DeviceIdType.MESH
        )
    pl.semaphore_wait(barrier, 3)

    forward = chips // 2
    backward = chips - 1 - forward
    rows = in_ref.shape[0]
    cut = (rows // 2 + 15) // 16 * 16
    pieces = ((0, cut), (cut, rows - cut))
    ring_ahead, ring_behind, across = 0, forward, forward + backward

    def copy(source, slot, piece, index, peer):
        start, size = pieces[piece]
        target = out_ref.at[slot, pl.ds(start, size), :]
        taken = target if source is None else source.at[pl.ds(start, size), :]
        return pltpu.make_async_remote_copy(
            src_ref=taken,
            dst_ref=target,
            send_sem=send.at[index, piece],
            recv_sem=got.at[index, piece],
            device_id={"slc": peer},
            device_id_type=pl.DeviceIdType.MESH,
        )

    local = pltpu.make_async_copy(in_ref, out_ref.at[me], local_sem)
    sent = []

    def launch(*what):
        one = copy(*what)
        one.start()
        sent.append(one)

    for piece in range(2):
        launch(in_ref, me, piece, ring_ahead, ahead)
        launch(in_ref, me, piece, ring_behind, behind)
    for piece in range(2):
        launch(in_ref, me, piece, across, twin)
    local.start()
    for step in range(forward):
        for piece in range(2):
            slot = at(spot - 1 - step)
            copy(None, slot, piece, ring_ahead + step, behind).wait_recv()
            if step + 1 < forward:
                launch(None, slot, piece, ring_ahead + step + 1, ahead)
            launch(None, slot, piece, across + 1 + step, twin)
            if step < backward:
                slot = at(spot + 1 + step)
                copy(None, slot, piece, ring_behind + step, ahead).wait_recv()
                if step + 1 < backward:
                    launch(None, slot, piece, ring_behind + step + 1, behind)
                launch(None, slot, piece, across + 1 + forward + step, twin)
    for index in range(chips):
        for piece in range(2):
            if index == 0:
                slot = twin
            elif index <= forward:
                slot = at(spot - index) + 1 - 2 * core
            else:
                slot = at(spot + index - forward) + 1 - 2 * core
            copy(None, slot, piece, across + index, twin).wait_recv()
    for one in sent:
        one.wait_send()
    local.wait()


def apply_kernel(
    width, share, kernels_ref, phase_ref, cos_ref, sin_ref, maps_ref, out_ref, high, low
):
    @pl.when(pl.program_id(0) == 0)
    def _():
        phase = phase_ref[...]
        phase_high = phase.astype(jnp.bfloat16)
        phase_low = (phase - phase_high.astype(jnp.float32)).astype(jnp.bfloat16)
        from_lane = lax.broadcasted_iota(jnp.int32, (phase.shape[1], width * PAIR), 0)
        to_lane = lax.broadcasted_iota(jnp.int32, (phase.shape[1], width * PAIR), 1)
        spread = (from_lane == to_lane // COILS).astype(jnp.float32).astype(jnp.bfloat16)
        row = lax.broadcasted_iota(jnp.int32, high.shape, 0)
        lane = lax.broadcasted_iota(jnp.int32, high.shape, 1)
        same = row % COILS == lane % COILS
        high[...] = jnp.where(same, dot_nn(phase_high, spread), 0.0).astype(jnp.bfloat16)
        low[...] = jnp.where(same, dot_nn(phase_low, spread), 0.0).astype(jnp.bfloat16)

    kernels = kernels_ref[0]
    image = (dot_nn(kernels, high[...]) + dot_nn(kernels, low[...])).astype(jnp.bfloat16)
    cos_x = cos_ref[...]
    sin_x = sin_ref[...]
    length = cos_x.shape[1]
    for y in range(width):
        real = maps_ref[y, 0, 0]
        imag = maps_ref[y, 0, 1]
        both = jnp.concatenate(
            [jnp.concatenate([real, imag], axis=1), jnp.concatenate([-imag, real], axis=1)], axis=0
        )
        mixed = dot_nn(image[:, y * PAIR : (y + 1) * PAIR], both)
        mixed_real = mixed[:, :length]
        mixed_imag = mixed[:, length:]
        out_real = mixed_real * cos_x - mixed_imag * sin_x
        out_imag = mixed_real * sin_x + mixed_imag * cos_x
        for ri, value in ((0, out_real), (1, out_imag)):
            total = value[:share]
            for p in range(1, SPAN):
                total = total + value[p * share : (p + 1) * share]
            out_ref[y, 0, ri] = total.astype(jnp.bfloat16)


def shards(basis, picks, coil_maps):
    n_col = lax.axis_size("col")
    share = COILS // n_col
    length = coil_maps.shape[-1]
    width = coil_maps.shape[0]
    slices = coil_maps.shape[1]
    rows, block = basis.shape[2:]
    keep = picks.shape[1]
    factor = 1.0 / (2.0 * keep * n_col * KSIZE * KSIZE)
    high_rows = SPAN * share
    lanes = SLOTS * PAIR
    vmem = pl.BlockSpec(memory_space=pltpu.VMEM)
    bf16 = jnp.bfloat16

    windows = jnp.transpose(basis[0], (0, 2, 1))
    col = lax.axis_index("col").astype(jnp.int32).reshape(1)
    part = jax.ShapeDtypeStruct((high_rows, lanes), jnp.float32)
    own, other = pl.pallas_call(
        functools.partial(gram_kernel, factor, share),
        out_shape=(part, jax.ShapeDtypeStruct((high_rows, lanes), bf16)),
        in_specs=[
            pl.BlockSpec(memory_space=pltpu.SMEM),
            pl.BlockSpec(memory_space=pl.ANY),
            vmem,
        ],
        out_specs=(vmem, vmem),
        scratch_shapes=[
            pltpu.VMEM((2, block, rows), bf16),
            pltpu.SemaphoreType.DMA((2,)),
            pltpu.VMEM((keep, block), bf16),
            pltpu.VMEM((rows, rows), bf16),
            pltpu.VMEM((2, rows, keep), bf16),
            pltpu.VMEM((KSIZE, (KSIZE + 2) * PAIR, keep), bf16),
            pltpu.VMEM((KSIZE, (KSIZE + 2) * PAIR, keep), bf16),
            pltpu.VMEM((KSIZE, KSIZE * COILS, keep), bf16),
            pltpu.VMEM((KSIZE, KSIZE * COILS, keep), bf16),
            pltpu.VMEM((KSIZE, KSIZE * COILS, lanes), jnp.float32),
        ],
        compiler_params=pltpu.CompilerParams(vmem_limit_bytes=60 * 2**20),
        name="gram",
    )(col, windows, picks.reshape(keep, 1))

    got = lax.ppermute(other, "col", [(i, n_col - 1 - i) for i in range(n_col)])
    kernels = pl.pallas_call(
        join_kernel,
        out_shape=jax.ShapeDtypeStruct((high_rows, lanes), bf16),
        in_specs=[vmem, vmem],
        out_specs=vmem,
        scratch_shapes=[pltpu.VMEM((high_rows, lanes), jnp.float32)],
        name="join",
    )(own, got)
    n_slc = lax.axis_size("slc")
    gathered = pl.pallas_call(
        spread_kernel,
        out_shape=jax.ShapeDtypeStruct((n_slc, high_rows, lanes), bf16),
        in_specs=[vmem],
        out_specs=pl.BlockSpec(memory_space=pl.ANY),
        scratch_shapes=[
            pltpu.SemaphoreType.DMA,
            pltpu.SemaphoreType.DMA((n_slc - 1, 2)),
            pltpu.SemaphoreType.DMA((n_slc - 1, 2)),
        ],
        compiler_params=pltpu.CompilerParams(collective_id=0, has_side_effects=True),
        name="spread",
    )(kernels)

    row = lax.broadcasted_iota(jnp.int32, (lanes, 128), 0)
    lane = lax.broadcasted_iota(jnp.int32, (lanes, 128), 1)
    slot = row // PAIR
    offset = jnp.where(slot == SPAN, 0, slot - CENTRE)
    column = lax.axis_index("slc") * width + lane // 2
    angle = (offset * column % length).astype(jnp.float32) * (2.0 * math.pi / length)
    from_imag = row // COILS % 2
    to_imag = lane % 2
    phase = jnp.where(from_imag == to_imag, jnp.cos(angle), jnp.sin(angle))
    phase = jnp.where((from_imag == 1) & (to_imag == 0), -phase, phase)

    spot = lax.broadcasted_iota(jnp.int32, (high_rows, length), 0) // share - CENTRE
    place = lax.broadcasted_iota(jnp.int32, (high_rows, length), 1)
    turn = (spot * place % length).astype(jnp.float32) * (2.0 * math.pi / length)

    whole = lambda shape: pl.BlockSpec(shape, lambda s: (0,) * len(shape))
    return pl.pallas_call(
        functools.partial(apply_kernel, width, share),
        grid=(slices,),
        out_shape=jax.ShapeDtypeStruct((width, slices, 2, share, length), bf16),
        in_specs=[
            pl.BlockSpec((1, high_rows, lanes), lambda s: (s, 0, 0)),
            whole((lanes, 128)),
            whole((high_rows, length)),
            whole((high_rows, length)),
            pl.BlockSpec((width, 1, 2, COILS, length), lambda s: (0, s, 0, 0, 0)),
        ],
        out_specs=pl.BlockSpec((width, 1, 2, share, length), lambda s: (0, s, 0, 0, 0)),
        scratch_shapes=[
            pltpu.VMEM((lanes, width * PAIR), bf16),
            pltpu.VMEM((lanes, width * PAIR), bf16),
        ],
        name="apply",
    )(gathered, phase, jnp.cos(turn), jnp.sin(turn), coil_maps)


def solution(mesh):
    placed = (P("slc", None, None, "col"), P("slc", "col"), P("slc", None, None, None, None))
    return jax.shard_map(
        shards,
        mesh=mesh,
        in_specs=placed,
        out_specs=P("slc", None, None, "col", None),
        check_vma=False,
    )
```
